32 devices in a mesh: energy: 16 (over z, x, core), mom: 2 (over y).
Axes of the slice: x: 2, y: 2, z: 4, core: 2. Of those that a mesh axis runs over, the one named last changes fastest.
Arguments:
- sigma_in: float32 [64, 2, 2, 256, 256], P('energy', 'mom'), may hold values from -0.1875 to 0.1875
- hamiltonian: float32 [2, 2, 256, 256], P('mom'), may hold values from -0.375 to 0.375
- coupling: float32 [2, 256, 256], P('mom'), may hold values from -0.1875 to 0.1875
- energies: float32 [64], replicated, may hold values from 1.4 to 2, as said below
- counts: int32 [64], replicated, may hold values from 2 to 4, as said below
- strengths: float32 [16], replicated, may hold values from 0.05625 to 0.1875
- offsets: int32 [16], replicated, may hold values from 0 to 1
Outputs:
- sigma_next: float32 [64, 2, 2, 256, 256], P('energy', 'mom')
The draws below stay inside these ranges and needn't reach their ends.
Inputs may be any that keep to these rules, and one draw needn't show every extreme that they name: `energies`: increasing along the grid. `counts`: each point needs either 2 or 4 sweeps, and some point needs 4.
All inputs are finite; a program needn't handle non-finite values.
Results may differ from the reference program's by a relative error of at most 0.0003.
Values sent between devices are 32-bit elements; how exact they have to be, the bound alone decides.
A program may use at most 64 MiB of HBM per device.

```python
import math
import jax
import jax.numpy as jnp
from jax import lax

M = 256
E_DEV = 4
S_LO = 2
S_MAX = 4
NQ = 16
E_TOT = 64
K = 2
N_ENERGY = 16
N_MOM = 2


def draw_energies(key, part):
    key_gaps, key_block = jax.random.split(jax.random.fold_in(key, 3))
    blocks = E_TOT // E_DEV
    wide_gap = min(0.03, 0.24 / E_DEV)
    planted = jax.random.randint(key_block, (), 0, blocks)
    gap_index = jnp.arange(E_TOT - 1, dtype=jnp.int32)
    inside = (gap_index >= planted * E_DEV) & (gap_index < planted * E_DEV + E_DEV - 1)
    raw_gaps = jax.random.uniform(key_gaps, (E_TOT - 1,), jnp.float32, 0.3, 1.0)
    raw_gaps = jnp.where(inside, 0.0, raw_gaps)
    remaining = 0.58 - wide_gap * (E_DEV - 1)
    gaps = jnp.where(inside, wide_gap, raw_gaps * (remaining / jnp.sum(raw_gaps)))
    steps_taken = jnp.concatenate([jnp.zeros((1,), jnp.float32), jnp.cumsum(gaps)])
    return 1.405 + steps_taken


def draw_counts(key, part):
    key_slow, key_place = jax.random.split(jax.random.fold_in(key, 7))
    index = jnp.arange(E_TOT, dtype=jnp.int32)
    low_band = max(E_TOT // 4, 1)
    chance = jnp.where(index < low_band, 10, 1)
    rolled = jax.random.randint(key_slow, (E_TOT,), 0, 20)
    forced = jax.random.randint(key_place, (), 0, low_band)
    slowed = (rolled < chance) | (index == forced)
    return jnp.where(slowed, S_MAX, S_LO).astype(jnp.int32)


def with_ends(drawn, key, smallest, top_value):
    spot = [jax.random.randint(jax.random.fold_in(key, axis), (), 0, length) for axis, length in enumerate(drawn.shape)]
    longest = drawn.shape.index(max(drawn.shape))
    beside = spot[:longest] + [(spot[longest] + 1) % drawn.shape[longest]] + spot[longest + 1:]
    return drawn.at[tuple(spot)].set(smallest).at[tuple(beside)].set(top_value)


def level_of(rng, dims, shards, low, largest):
    gain, own = 1.0, jax.random.fold_in(rng, 6)
    for dim, blocks in shards:
        draws = jnp.exp(jax.random.uniform(jax.random.fold_in(own, dim), (blocks,), jnp.float32, low / len(shards), largest / len(shards)))
        gain = gain * jnp.repeat(draws, dims[dim] // blocks).reshape([-1 if axis == dim else 1 for axis in range(len(dims))])
    return gain


def normal_values(rng, dims, spread, most, shards=(), kind=jnp.bfloat16):
    values = jax.random.normal(rng, dims, jnp.float32) * spread
    if len(shards) > 0:
        values = level_of(rng, dims, shards, -0.22, 0.18) * values
    return jnp.clip(values, min=-most, max=most).astype(kind)


def setup_inputs(seed: int = 0) -> dict:
    seeds = jax.random.split(jax.random.key(seed), 8)
    sigma_in = normal_values(seeds[0], (E_TOT, K, 2, M, M), (4 * M) ** -0.5, 0.1875, ((0, 16), (1, 2)), jnp.float32)
    hamiltonian = normal_values(seeds[1], (K, 2, M, M), M ** -0.5, 0.375, ((0, 2),), jnp.float32)
    coupling = normal_values(seeds[2], (K, M, M), (4 * M) ** -0.5, 0.1875, ((0, 2),), jnp.float32)
    energies = draw_energies(jax.random.fold_in(seeds[7], 71), 0)
    counts = draw_counts(jax.random.fold_in(seeds[7], 71), 0)
    strengths = jnp.clip(jnp.exp(jax.random.uniform(seeds[5], (NQ,), jnp.float32, math.log(0.05625), math.log(0.1875))), 0.05625, 0.1875)
    offsets = with_ends(jax.random.randint(seeds[6], (NQ,), 0, N_MOM), jax.random.fold_in(seeds[6], 1), 0, N_MOM - 1).astype(jnp.int32)
    return dict(sigma_in=sigma_in, hamiltonian=hamiltonian, coupling=coupling, energies=energies, counts=counts, strengths=strengths, offsets=offsets)


PRECISE = lax.Precision.HIGHEST
MIX_RATE = 0.6
PHONON = 0.1
BROADENING = 0.02


def product(left_side, right_side):
    return jnp.dot(left_side, right_side, precision=PRECISE, preferred_element_type=jnp.float32)


def invert(matrix, energy, sweeps):
    identity = jnp.eye(matrix.shape[0], dtype=jnp.float32)
    estimate = identity / energy
    for sweep_index in range(S_MAX):
        updated = 2.0 * estimate - product(estimate, product(matrix, estimate))
        estimate = jnp.where(sweep_index < sweeps, updated, estimate)
    return estimate


def solve_point(ham_block, coupling_block, sigma_pair, energy, sweeps):
    identity = jnp.eye(ham_block.shape[1], dtype=jnp.float32)
    left_matrix = energy * identity - ham_block[0] - sigma_pair[0]
    left_inverse = invert(left_matrix, energy, sweeps)
    inverse_coupled = product(left_inverse, coupling_block)
    coupled_inverse = product(coupling_block.T, left_inverse)
    right_matrix = energy * identity - ham_block[1] - sigma_pair[1] - product(coupling_block.T, inverse_coupled)
    right_green = invert(right_matrix, energy, sweeps)
    left_green = left_inverse + product(product(inverse_coupled, right_green), coupled_inverse)
    return jnp.stack([left_green, right_green])


def lorentz(offset):
    scaled = offset / BROADENING
    return 1.0 / (1.0 + scaled * scaled)


def build_kernel(row_energy, column_energy):
    spacing = row_energy[:, None] - column_energy[None, :]
    kernel = lorentz(spacing - PHONON) + lorentz(spacing + PHONON)
    return kernel / jnp.sum(kernel, axis=1, keepdims=True)


def reference(sigma_in, hamiltonian, coupling, energies, counts, strengths, offsets):
    def per_energy(held_point):
        sigma_row, energy, sweeps = held_point

        def per_momentum(ham_block, coupling_block, sigma_pair):
            return solve_point(ham_block, coupling_block, sigma_pair, energy, sweeps)

        return jax.vmap(per_momentum)(hamiltonian, coupling, sigma_row)

    green_blocks = lax.map(per_energy, (sigma_in, energies, counts))
    shift_index = jnp.arange(K, dtype=jnp.int32)
    weights = jnp.sum(strengths[:, None] * (offsets[:, None] == shift_index[None, :]).astype(jnp.float32), axis=0)
    kernel = build_kernel(energies, energies)
    piece_width = 2 * M * M // N_ENERGY
    flattened = green_blocks.reshape(E_TOT, K, 2 * M * M)

    def per_block(block_index):
        element_block = lax.dynamic_slice_in_dim(flattened, block_index * piece_width, piece_width, 2)
        mixed_sum = weights[0] * element_block
        for offset_step in range(1, K):
            mixed_sum = mixed_sum + weights[offset_step] * jnp.roll(element_block, offset_step, axis=1)
        return jnp.einsum("ae,ekf->akf", kernel, mixed_sum, precision=PRECISE)

    pieces = lax.map(per_block, jnp.arange(N_ENERGY, dtype=jnp.int32))
    sigma_new = jnp.transpose(pieces, (1, 2, 0, 3)).reshape(sigma_in.shape)
    return (1.0 - MIX_RATE) * sigma_in + MIX_RATE * sigma_new
```

```python
import functools

import jax
import jax.numpy as jnp
from jax import lax
from jax.experimental import pallas as pl
from jax.experimental.pallas import tpu as pltpu
from jax.sharding import PartitionSpec as P

PRECISE = lax.Precision.HIGHEST
MIX_RATE = 0.6
PHONON = 0.1
BROADENING = 0.02


def shifted(value, axis, steps):
    count = lax.axis_size(axis)
    pairs = [(source, (source + steps) % count) for source in range(count)]
    return lax.ppermute(value, axis, pairs)


def product(left_side, right_side):
    return jnp.dot(left_side, right_side, precision=PRECISE, preferred_element_type=jnp.float32)


def invert(matrix, energy, sweeps):
    identity = jnp.eye(matrix.shape[0], dtype=jnp.float32)

    def keep_going(carried):
        return carried[0] < sweeps

    def sweep(carried):
        estimate = carried[1]
        return (carried[0] + 1, 2.0 * estimate - product(estimate, product(matrix, estimate)))

    return lax.while_loop(keep_going, sweep, (jnp.int32(0), identity / energy))[1]


def solve_point(ham_block, coupling_block, sigma_pair, energy, sweeps):
    identity = jnp.eye(ham_block.shape[1], dtype=jnp.float32)
    left_matrix = energy * identity - ham_block[0] - sigma_pair[0]
    left_inverse = invert(left_matrix, energy, sweeps)
    inverse_coupled = product(left_inverse, coupling_block)
    coupled_inverse = product(coupling_block.T, left_inverse)
    right_matrix = (
        energy * identity
        - ham_block[1]
        - sigma_pair[1]
        - product(coupling_block.T, inverse_coupled)
    )
    right_green = invert(right_matrix, energy, sweeps)
    left_green = left_inverse + product(product(inverse_coupled, right_green), coupled_inverse)
    return jnp.stack([left_green, right_green])


def lorentz(offset):
    scaled = offset / BROADENING
    return 1.0 / (1.0 + scaled * scaled)


def build_kernel(row_energy, column_energy):
    spacing = row_energy[:, None] - column_energy[None, :]
    kernel = lorentz(spacing - PHONON) + lorentz(spacing + PHONON)
    return kernel / jnp.sum(kernel, axis=1, keepdims=True)


def plain_body(sigma_in, hamiltonian, coupling, energies, counts, strengths, offsets):
    points = sigma_in.shape[0]
    order = sigma_in.shape[3]
    ranks = lax.axis_size("energy")
    moments = lax.axis_size("mom")
    my_rank = lax.axis_index("energy")
    own_energy = lax.dynamic_slice_in_dim(energies, my_rank * points, points)
    own_count = lax.dynamic_slice_in_dim(counts, my_rank * points, points)
    blocks = sigma_in[:, 0]

    def solve_held(held_point):
        return solve_point(hamiltonian[0], coupling[0], held_point[0], held_point[1], held_point[2])

    green_blocks = lax.map(solve_held, (blocks, own_energy, own_count))
    shift_index = jnp.arange(moments, dtype=jnp.int32)
    weights = jnp.sum(
        strengths[:, None] * (offsets[:, None] == shift_index[None, :]).astype(jnp.float32), axis=0
    )
    kernel = build_kernel(energies, energies)
    piece_width = 2 * order * order // ranks
    spread = green_blocks.reshape(points, ranks, moments, piece_width // moments)
    column = lax.all_to_all(spread, "energy", split_axis=1, concat_axis=0, tiled=True)[:, 0]
    rows_all = column.shape[0]
    flat_column = column.reshape(rows_all, -1)
    mixed_sum = weights[0] * flat_column
    for offset_step in range(1, moments):
        mixed_sum = mixed_sum + weights[offset_step] * shifted(flat_column, "mom", offset_step)
    sigma_part = product(kernel, mixed_sum).reshape(column.shape)
    result = lax.all_to_all(sigma_part[:, None], "energy", split_axis=0, concat_axis=1, tiled=True)
    sigma_new = result.reshape(sigma_in.shape)
    return (1.0 - MIX_RATE) * sigma_in + MIX_RATE * sigma_new


SUBLANES = 8
TOGETHER = 2
MESH_ID = pl.DeviceIdType.MESH


def split(value):
    high = value.astype(jnp.bfloat16)
    return high, (value - high.astype(jnp.float32)).astype(jnp.bfloat16)


def left_parts(value):
    high, low = split(value)
    return jnp.concatenate([high, low, high], axis=1)


def right_parts(value):
    high, low = split(value)
    return jnp.concatenate([high, high, low], axis=0)


def multiply(left_side, right_side):
    return jnp.dot(left_side, right_side, preferred_element_type=jnp.float32)


def series(ratios, energies, counts, identity):
    order = identity.shape[0]
    squares = [multiply(left_parts(r), right_parts(r)) for r in ratios]
    totals = [identity + r for r in ratios]
    for sweep in (1, 2, 3):
        rights = [right_parts(s) for s in squares]
        if sweep < 3:
            both = [
                multiply(jnp.concatenate([left_parts(t), left_parts(s)], axis=0), q)
                for t, s, q in zip(totals, squares, rights)
            ]
            added = [b[:order] for b in both]
            squares = [b[order:] for b in both]
        else:
            added = [multiply(left_parts(t), q) for t, q in zip(totals, rights)]
        totals = [jnp.where(sweep < c, t + a, t) for t, a, c in zip(totals, added, counts)]
    return [t * (1.0 / e) for t, e in zip(totals, energies)]


def kernel(
    ranks, moments, points, order, held,
    energy_ref, count_ref, strength_ref, offset_ref, sigma_ref, ham_ref, coupling_ref,
    out_ref,
    green, gathered, mixed_out, wide, across, across_t,
    send_first, recv_first, send_second, recv_second,
):
    devices = ranks * moments
    total = ranks * points
    my_rank = lax.axis_index("energy")
    my_moment = lax.axis_index("mom")
    me = my_rank * moments + my_moment
    barrier = pltpu.get_barrier_semaphore()

    def greet(index, carried):
        other = lax.rem(me + index, devices)
        pl.semaphore_signal(
            barrier, inc=1,
            device_id={"energy": other // moments, "mom": lax.rem(other, moments)},
            device_id_type=MESH_ID,
        )
        return carried

    lax.fori_loop(1, devices, greet, 0)

    span = total * SUBLANES
    column = lax.broadcasted_iota(jnp.int32, (SUBLANES, span), 1)
    lane_slot = lax.rem(column, SUBLANES)
    lane_point = lax.div(column, SUBLANES)
    same = lane_slot == lax.broadcasted_iota(jnp.int32, (SUBLANES, span), 0)

    def place(index, carried):
        return jnp.where(lane_point == index, energy_ref[index], carried)

    column_energy = lax.fori_loop(0, total, place, jnp.zeros((SUBLANES, span), jnp.float32))

    def build(index, carried):
        spacing = energy_ref[index] - column_energy
        row = lorentz(spacing - PHONON) + lorentz(spacing + PHONON)
        row = jnp.where(same, row, 0.0)
        row = row / jnp.sum(row, axis=1, keepdims=True)
        wide[pl.ds(pl.multiple_of(index * SUBLANES, SUBLANES), SUBLANES), :] = row
        return carried

    lax.fori_loop(0, total, build, 0)
    weights = []
    for step in range(moments):
        weight = jnp.float32(0.0)
        for transfer in range(strength_ref.shape[0]):
            weight = weight + jnp.where(offset_ref[transfer] == step, strength_ref[transfer], 0.0)
        weights.append(weight)

    across[...] = right_parts(coupling_ref[...])
    across_t[...] = left_parts(coupling_ref[...].T)
    row_index = lax.broadcasted_iota(jnp.int32, (order, order), 0)
    identity = (row_index == lax.broadcasted_iota(jnp.int32, (order, order), 1)).astype(jnp.float32)
    pl.semaphore_wait(barrier, devices - 1)

    half = devices // 2

    def first_copy(point, other):
        return pltpu.make_async_remote_copy(
            src_ref=green.at[point, pl.ds(other * held, held)],
            dst_ref=gathered.at[my_moment, :, my_rank * points + point],
            send_sem=send_first,
            recv_sem=recv_first,
            device_id={"energy": other // moments, "mom": lax.rem(other, moments)},
            device_id_type=MESH_ID,
        )

    def solve(group, carried):
        chosen = [group * TOGETHER + index for index in range(TOGETHER)]
        energies = [energy_ref[my_rank * points + point] for point in chosen]
        counts = [count_ref[my_rank * points + point] for point in chosen]
        ratios = [(ham_ref[0] + sigma_ref[point, 0]) * (1.0 / e) for point, e in zip(chosen, energies)]
        left_inverses = series(ratios, energies, counts, identity)
        coupled = [multiply(left_parts(x), across[...]) for x in left_inverses]
        backs = [multiply(across_t[...], right_parts(x)) for x in left_inverses]
        folds = [multiply(across_t[...], right_parts(x)) for x in coupled]
        ratios = [
            (ham_ref[1] + sigma_ref[point, 1] + fold) * (1.0 / e)
            for point, e, fold in zip(chosen, energies, folds)
        ]
        right_greens = series(ratios, energies, counts, identity)
        inner = [multiply(left_parts(c), right_parts(x)) for c, x in zip(coupled, right_greens)]
        left_greens = [
            x + multiply(left_parts(i), right_parts(b)) for x, i, b in zip(left_inverses, inner, backs)
        ]
        tiles = order // SUBLANES
        for point, left_green, right_green in zip(chosen, left_greens, right_greens):
            green[point, :tiles] = left_green.reshape(tiles, SUBLANES, order)
            green[point, tiles:] = right_green.reshape(tiles, SUBLANES, order)
        for point in chosen:
            pltpu.make_async_copy(
                green.at[point, pl.ds(me * held, held)],
                gathered.at[my_moment, :, my_rank * points + point],
                recv_first,
            ).start()

            def send(index, inner_carried, point=point):
                away = (index + 1) // 2
                offset = half + away * (2 * lax.rem(index, 2) - 1)
                first_copy(point, lax.rem(me + offset, devices)).start()
                return inner_carried

            lax.fori_loop(0, devices - 1, send, 0)
        return carried

    lax.fori_loop(0, points // TOGETHER, solve, 0)

    pltpu.make_async_copy(gathered, gathered, recv_first).wait()

    wide_parts = left_parts(wide[...])
    for turn in range(moments):
        moment = lax.rem(my_moment + 1 + turn, moments)
        for piece in range(held):
            scattered = weights[0] * gathered[moment, piece]
            for step in range(1, moments):
                source = lax.rem(moment - step + moments, moments)
                scattered = scattered + weights[step] * gathered[source, piece]
            result = multiply(wide_parts, right_parts(scattered.reshape(span, order)))
            mixed_out[moment, piece] = result.reshape(total, SUBLANES, order)

            def give_back(index, carried, moment=moment, piece=piece):
                away = (index + 1) // 2
                offset = ranks // 2 + away * (2 * lax.rem(index, 2) - 1)
                rank = lax.rem(my_rank + offset, ranks)
                pltpu.make_async_remote_copy(
                    src_ref=mixed_out.at[moment, piece, pl.ds(rank * points, points)],
                    dst_ref=out_ref.at[:, me * held + piece],
                    send_sem=send_second,
                    recv_sem=recv_second,
                    device_id={"energy": rank, "mom": moment},
                    device_id_type=MESH_ID,
                ).start()
                return carried

            if turn < moments - 1:
                lax.fori_loop(0, ranks, give_back, 0)
            else:
                lax.fori_loop(0, ranks - 1, give_back, 0)
                pltpu.make_async_copy(
                    mixed_out.at[my_moment, piece, pl.ds(my_rank * points, points)],
                    out_ref.at[:, me * held + piece],
                    recv_second,
                ).start()

    pltpu.make_async_copy(out_ref, out_ref, recv_second).wait()
    sent = green.at[:, pl.ds(0, (devices - 1) * held)]
    pltpu.make_async_copy(sent, sent, send_first).wait()
    pltpu.make_async_copy(sent, sent, send_second).wait()


def fused_body(sigma_in, hamiltonian, coupling, energies, counts, strengths, offsets):
    points, order = sigma_in.shape[0], sigma_in.shape[3]
    ranks = lax.axis_size("energy")
    moments = lax.axis_size("mom")
    tiles = 2 * order // SUBLANES
    held = tiles // (ranks * moments)
    span = ranks * points * SUBLANES
    smem = pl.BlockSpec(memory_space=pltpu.SMEM)
    vmem = pl.BlockSpec(memory_space=pltpu.VMEM)
    sigma_new = pl.pallas_call(
        functools.partial(kernel, ranks, moments, points, order, held),
        out_shape=jax.ShapeDtypeStruct((points, tiles, SUBLANES, order), jnp.float32),
        in_specs=[smem] * 4 + [vmem] * 3,
        out_specs=pl.BlockSpec(memory_space=pl.ANY),
        scratch_shapes=[
            pltpu.VMEM((points, tiles, SUBLANES, order), jnp.float32),
            pltpu.VMEM((moments, held, ranks * points, SUBLANES, order), jnp.float32),
            pltpu.VMEM((moments, held, ranks * points, SUBLANES, order), jnp.float32),
            pltpu.VMEM((span, span), jnp.float32),
            pltpu.VMEM((3 * order, order), jnp.bfloat16),
            pltpu.VMEM((order, 3 * order), jnp.bfloat16),
            pltpu.SemaphoreType.DMA,
            pltpu.SemaphoreType.DMA,
            pltpu.SemaphoreType.DMA,
            pltpu.SemaphoreType.DMA,
        ],
        compiler_params=pltpu.CompilerParams(
            collective_id=0, has_side_effects=True, vmem_limit_bytes=60 * 1024 * 1024
        ),
        name="green_and_scatter",
    )(energies, counts, strengths, offsets, sigma_in[:, 0], hamiltonian[0], coupling[0])
    return (1.0 - MIX_RATE) * sigma_in + MIX_RATE * sigma_new.reshape(sigma_in.shape)


def body(sigma_in, hamiltonian, coupling, energies, counts, strengths, offsets):
    devices = lax.axis_size("energy") * lax.axis_size("mom")
    tiles = 2 * sigma_in.shape[3] // SUBLANES
    fits = tiles % devices == 0 and devices % 2 == 0 and sigma_in.shape[0] % TOGETHER == 0
    chosen = fused_body if fits else plain_body
    return chosen(sigma_in, hamiltonian, coupling, energies, counts, strengths, offsets)


def solution(mesh):
    placed = (
        P("energy", "mom", None, None, None),
        P("mom", None, None, None),
        P("mom", None, None),
        P(),
        P(),
        P(),
        P(),
    )
    return jax.shard_map(
        body,
        mesh=mesh,
        in_specs=placed,
        out_specs=P("energy", "mom", None, None, None),
        check_vma=False,
    )
```

```python
import functools

import jax
import jax.numpy as jnp
from jax import lax
from jax.experimental import pallas as pl
from jax.experimental.pallas import tpu as pltpu
from jax.sharding import PartitionSpec as P

PRECISE = lax.Precision.HIGHEST
MIX_RATE = 0.6
PHONON = 0.1
BROADENING = 0.02


def shifted(value, axis, steps):
    count = lax.axis_size(axis)
    pairs = [(source, (source + steps) % count) for source in range(count)]
    return lax.ppermute(value, axis, pairs)


def product(left_side, right_side):
    return jnp.dot(left_side, right_side, precision=PRECISE, preferred_element_type=jnp.float32)


def invert(matrix, energy, sweeps):
    identity = jnp.eye(matrix.shape[0], dtype=jnp.float32)

    def keep_going(carried):
        return carried[0] < sweeps

    def sweep(carried):
        estimate = carried[1]
        return (carried[0] + 1, 2.0 * estimate - product(estimate, product(matrix, estimate)))

    return lax.while_loop(keep_going, sweep, (jnp.int32(0), identity / energy))[1]


def solve_point(ham_block, coupling_block, sigma_pair, energy, sweeps):
    identity = jnp.eye(ham_block.shape[1], dtype=jnp.float32)
    left_matrix = energy * identity - ham_block[0] - sigma_pair[0]
    left_inverse = invert(left_matrix, energy, sweeps)
    inverse_coupled = product(left_inverse, coupling_block)
    coupled_inverse = product(coupling_block.T, left_inverse)
    right_matrix = (
        energy * identity
        - ham_block[1]
        - sigma_pair[1]
        - product(coupling_block.T, inverse_coupled)
    )
    right_green = invert(right_matrix, energy, sweeps)
    left_green = left_inverse + product(product(inverse_coupled, right_green), coupled_inverse)
    return jnp.stack([left_green, right_green])


def lorentz(offset):
    scaled = offset / BROADENING
    return 1.0 / (1.0 + scaled * scaled)


def build_kernel(row_energy, column_energy):
    spacing = row_energy[:, None] - column_energy[None, :]
    kernel = lorentz(spacing - PHONON) + lorentz(spacing + PHONON)
    return kernel / jnp.sum(kernel, axis=1, keepdims=True)


def plain_body(sigma_in, hamiltonian, coupling, energies, counts, strengths, offsets):
    points = sigma_in.shape[0]
    order = sigma_in.shape[3]
    ranks = lax.axis_size("energy")
    moments = lax.axis_size("mom")
    my_rank = lax.axis_index("energy")
    own_energy = lax.dynamic_slice_in_dim(energies, my_rank * points, points)
    own_count = lax.dynamic_slice_in_dim(counts, my_rank * points, points)
    blocks = sigma_in[:, 0]

    def solve_held(held_point):
        return solve_point(hamiltonian[0], coupling[0], held_point[0], held_point[1], held_point[2])

    green_blocks = lax.map(solve_held, (blocks, own_energy, own_count))
    shift_index = jnp.arange(moments, dtype=jnp.int32)
    weights = jnp.sum(
        strengths[:, None] * (offsets[:, None] == shift_index[None, :]).astype(jnp.float32), axis=0
    )
    kernel = build_kernel(energies, energies)
    piece_width = 2 * order * order // ranks
    spread = green_blocks.reshape(points, ranks, moments, piece_width // moments)
    column = lax.all_to_all(spread, "energy", split_axis=1, concat_axis=0, tiled=True)[:, 0]
    rows_all = column.shape[0]
    flat_column = column.reshape(rows_all, -1)
    mixed_sum = weights[0] * flat_column
    for offset_step in range(1, moments):
        mixed_sum = mixed_sum + weights[offset_step] * shifted(flat_column, "mom", offset_step)
    sigma_part = product(kernel, mixed_sum).reshape(column.shape)
    result = lax.all_to_all(sigma_part[:, None], "energy", split_axis=0, concat_axis=1, tiled=True)
    sigma_new = result.reshape(sigma_in.shape)
    return (1.0 - MIX_RATE) * sigma_in + MIX_RATE * sigma_new


SUBLANES = 8
TOGETHER = 1
MESH_ID = pl.DeviceIdType.MESH


def split(value):
    high = value.astype(jnp.bfloat16)
    return high, (value - high.astype(jnp.float32)).astype(jnp.bfloat16)


def left_parts(value):
    high, low = split(value)
    return jnp.concatenate([high, low, high], axis=1)


def right_parts(value):
    high, low = split(value)
    return jnp.concatenate([high, high, low], axis=0)


def multiply(left_side, right_side):
    return jnp.dot(left_side, right_side, preferred_element_type=jnp.float32)


def series(ratios, energies, counts, identity):
    order = identity.shape[0]
    squares = [multiply(left_parts(r), right_parts(r)) for r in ratios]
    totals = [identity + r for r in ratios]
    for sweep in (1, 2, 3):
        rights = [right_parts(s) for s in squares]
        if sweep < 3:
            both = [
                multiply(jnp.concatenate([left_parts(t), left_parts(s)], axis=0), q)
                for t, s, q in zip(totals, squares, rights)
            ]
            added = [b[:order] for b in both]
            squares = [b[order:] for b in both]
        else:
            added = [multiply(left_parts(t), q) for t, q in zip(totals, rights)]
        totals = [jnp.where(sweep < c, t + a, t) for t, a, c in zip(totals, added, counts)]
    return [t * (1.0 / e) for t, e in zip(totals, energies)]


def kernel(
    ranks, moments, points, order, held,
    energy_ref, count_ref, strength_ref, offset_ref, sigma_ref, ham_ref, coupling_ref,
    out_ref,
    green, gathered, mixed_out, wide, across, across_t,
    send_first, recv_first, send_second, recv_second,
):
    devices = ranks * moments
    total = ranks * points
    my_rank = lax.axis_index("energy")
    my_moment = lax.axis_index("mom")
    me = my_rank * moments + my_moment
    barrier = pltpu.get_barrier_semaphore()

    def greet(index, carried):
        other = lax.rem(me + index, devices)
        pl.semaphore_signal(
            barrier, inc=1,
            device_id={"energy": other // moments, "mom": lax.rem(other, moments)},
            device_id_type=MESH_ID,
        )
        return carried

    lax.fori_loop(1, devices, greet, 0)

    across[...] = right_parts(coupling_ref[...])
    across_t[...] = left_parts(coupling_ref[...].T)
    row_index = lax.broadcasted_iota(jnp.int32, (order, order), 0)
    identity = (row_index == lax.broadcasted_iota(jnp.int32, (order, order), 1)).astype(jnp.float32)

    def place_of(other):
        return {"energy": other // moments, "mom": lax.rem(other, moments)}

    def give_first(source, landing, piece):
        pltpu.make_async_copy(source(me), landing, recv_first.at[piece]).start()

        def give(index, carried):
            other = lax.rem(me + index, devices)
            pltpu.make_async_remote_copy(
                src_ref=source(other),
                dst_ref=landing,
                send_sem=send_first,
                recv_sem=recv_first.at[piece],
                device_id=place_of(other),
                device_id_type=MESH_ID,
            ).start()
            return carried

        lax.fori_loop(1, devices, give, 0)

    def solve(group, carried):
        chosen = [group * TOGETHER + index for index in range(TOGETHER)]
        energies = [energy_ref[my_rank * points + point] for point in chosen]
        counts = [count_ref[my_rank * points + point] for point in chosen]
        ratios = [(ham_ref[0] + sigma_ref[point, 0]) * (1.0 / e) for point, e in zip(chosen, energies)]
        left_inverses = series(ratios, energies, counts, identity)
        coupled = [multiply(left_parts(x), across[...]) for x in left_inverses]
        backs = [multiply(across_t[...], right_parts(x)) for x in left_inverses]
        folds = [multiply(across_t[...], right_parts(x)) for x in coupled]
        ratios = [
            (ham_ref[1] + sigma_ref[point, 1] + fold) * (1.0 / e)
            for point, e, fold in zip(chosen, energies, folds)
        ]
        right_greens = series(ratios, energies, counts, identity)
        inner = [multiply(left_parts(c), right_parts(x)) for c, x in zip(coupled, right_greens)]
        left_greens = [
            x + multiply(left_parts(i), right_parts(b)) for x, i, b in zip(left_inverses, inner, backs)
        ]
        tiles = order // SUBLANES
        for point, left_green, right_green in zip(chosen, left_greens, right_greens):
            green[point, :tiles] = left_green.reshape(tiles, SUBLANES, order)
            green[point, tiles:] = right_green.reshape(tiles, SUBLANES, order)

        @pl.when(group == 0)
        def _():
            pl.semaphore_wait(barrier, devices - 1)

        for point in chosen:
            landing = gathered.at[my_moment, 0, my_rank * points + point]
            give_first(lambda other: green.at[point, other * held], landing, 0)
        return carried

    lax.fori_loop(0, points // TOGETHER, solve, 0)

    for piece in range(1, held):
        landing = gathered.at[my_moment, piece, pl.ds(my_rank * points, points)]
        give_first(lambda other: green.at[:, other * held + piece], landing, piece)

    span = total * SUBLANES
    column = lax.broadcasted_iota(jnp.int32, (SUBLANES, span), 1)
    lane_slot = lax.rem(column, SUBLANES)
    lane_point = lax.div(column, SUBLANES)
    same = lane_slot == lax.broadcasted_iota(jnp.int32, (SUBLANES, span), 0)

    def place(index, carried):
        return jnp.where(lane_point == index, energy_ref[index], carried)

    column_energy = lax.fori_loop(0, total, place, jnp.zeros((SUBLANES, span), jnp.float32))

    def build(index, carried):
        spacing = energy_ref[index] - column_energy
        row = lorentz(spacing - PHONON) + lorentz(spacing + PHONON)
        row = jnp.where(same, row, 0.0)
        row = row * (MIX_RATE / jnp.sum(row, axis=1, keepdims=True))
        wide[pl.ds(pl.multiple_of(index * SUBLANES, SUBLANES), SUBLANES), :] = row
        return carried

    lax.fori_loop(0, total, build, 0)
    weights = []
    for step in range(moments):
        weight = jnp.float32(0.0)
        for transfer in range(strength_ref.shape[0]):
            weight = weight + jnp.where(offset_ref[transfer] == step, strength_ref[transfer], 0.0)
        weights.append(weight)

    wide_parts = left_parts(wide[...])
    for piece in range(held):
        arrived = gathered.at[:, piece]
        pltpu.make_async_copy(arrived, arrived, recv_first.at[piece]).wait()
        for turn in range(moments):
            moment = lax.rem(my_moment + 1 + turn, moments)
            scattered = weights[0] * gathered[moment, piece]
            for step in range(1, moments):
                source = lax.rem(moment - step + moments, moments)
                scattered = scattered + weights[step] * gathered[source, piece]
            result = multiply(wide_parts, right_parts(scattered.reshape(span, order)))
            mixed_out[moment, piece] = result.reshape(total, SUBLANES, order)

            def give_back(index, carried, moment=moment, piece=piece):
                rank = lax.rem(my_rank + index, ranks)
                pltpu.make_async_remote_copy(
                    src_ref=mixed_out.at[moment, piece, pl.ds(rank * points, points)],
                    dst_ref=out_ref.at[:, me * held + piece],
                    send_sem=send_second,
                    recv_sem=recv_second,
                    device_id={"energy": rank, "mom": moment},
                    device_id_type=MESH_ID,
                ).start()
                return carried

            if turn < moments - 1:
                lax.fori_loop(0, ranks, give_back, 0)
            else:
                lax.fori_loop(1, ranks, give_back, 0)
                pltpu.make_async_copy(
                    mixed_out.at[my_moment, piece, pl.ds(my_rank * points, points)],
                    out_ref.at[:, me * held + piece],
                    recv_second,
                ).start()

    pltpu.make_async_copy(out_ref, out_ref, recv_second).wait()
    sent = green.at[:, pl.ds(0, (devices - 1) * held)]
    pltpu.make_async_copy(sent, sent, send_first).wait()
    pltpu.make_async_copy(sent, sent, send_second).wait()


def fused_body(sigma_in, hamiltonian, coupling, energies, counts, strengths, offsets):
    points, order = sigma_in.shape[0], sigma_in.shape[3]
    ranks = lax.axis_size("energy")
    moments = lax.axis_size("mom")
    tiles = 2 * order // SUBLANES
    held = tiles // (ranks * moments)
    span = ranks * points * SUBLANES
    smem = pl.BlockSpec(memory_space=pltpu.SMEM)
    vmem = pl.BlockSpec(memory_space=pltpu.VMEM)
    sigma_new = pl.pallas_call(
        functools.partial(kernel, ranks, moments, points, order, held),
        out_shape=jax.ShapeDtypeStruct((points, tiles, SUBLANES, order), jnp.float32),
        in_specs=[smem] * 4 + [vmem] * 3,
        out_specs=pl.BlockSpec(memory_space=pl.ANY),
        scratch_shapes=[
            pltpu.VMEM((points, tiles, SUBLANES, order), jnp.float32),
            pltpu.VMEM((moments, held, ranks * points, SUBLANES, order), jnp.float32),
            pltpu.VMEM((moments, held, ranks * points, SUBLANES, order), jnp.float32),
            pltpu.VMEM((span, span), jnp.float32),
            pltpu.VMEM((3 * order, order), jnp.bfloat16),
            pltpu.VMEM((order, 3 * order), jnp.bfloat16),
            pltpu.SemaphoreType.DMA,
            pltpu.SemaphoreType.DMA((held,)),
            pltpu.SemaphoreType.DMA,
            pltpu.SemaphoreType.DMA,
        ],
        compiler_params=pltpu.CompilerParams(
            collective_id=0, has_side_effects=True, vmem_limit_bytes=60 * 1024 * 1024
        ),
        name="green_and_scatter",
    )(energies, counts, strengths, offsets, sigma_in[:, 0], hamiltonian[0], coupling[0])
    return (1.0 - MIX_RATE) * sigma_in + sigma_new.reshape(sigma_in.shape)


def body(sigma_in, hamiltonian, coupling, energies, counts, strengths, offsets):
    devices = lax.axis_size("energy") * lax.axis_size("mom")
    tiles = 2 * sigma_in.shape[3] // SUBLANES
    fits = tiles % devices == 0 and devices % 2 == 0 and sigma_in.shape[0] % TOGETHER == 0
    chosen = fused_body if fits else plain_body
    return chosen(sigma_in, hamiltonian, coupling, energies, counts, strengths, offsets)


def solution(mesh):
    placed = (
        P("energy", "mom", None, None, None),
        P("mom", None, None, None),
        P("mom", None, None),
        P(),
        P(),
        P(),
        P(),
    )
    return jax.shard_map(
        body,
        mesh=mesh,
        in_specs=placed,
        out_specs=P("energy", "mom", None, None, None),
        check_vma=False,
    )
```

```python
import functools

import jax
import jax.numpy as jnp
from jax import lax
from jax.experimental import pallas as pl
from jax.experimental.pallas import tpu as pltpu
from jax.sharding import PartitionSpec as P

PRECISE = lax.Precision.HIGHEST
MIX_RATE = 0.6
PHONON = 0.1
BROADENING = 0.02


def shifted(value, axis, steps):
    count = lax.axis_size(axis)
    pairs = [(source, (source + steps) % count) for source in range(count)]
    return lax.ppermute(value, axis, pairs)


def product(left_side, right_side):
    return jnp.dot(left_side, right_side, precision=PRECISE, preferred_element_type=jnp.float32)


def invert(matrix, energy, sweeps):
    identity = jnp.eye(matrix.shape[0], dtype=jnp.float32)

    def keep_going(carried):
        return carried[0] < sweeps

    def sweep(carried):
        estimate = carried[1]
        return (carried[0] + 1, 2.0 * estimate - product(estimate, product(matrix, estimate)))

    return lax.while_loop(keep_going, sweep, (jnp.int32(0), identity / energy))[1]


def solve_point(ham_block, coupling_block, sigma_pair, energy, sweeps):
    identity = jnp.eye(ham_block.shape[1], dtype=jnp.float32)
    left_matrix = energy * identity - ham_block[0] - sigma_pair[0]
    left_inverse = invert(left_matrix, energy, sweeps)
    inverse_coupled = product(left_inverse, coupling_block)
    coupled_inverse = product(coupling_block.T, left_inverse)
    right_matrix = (
        energy * identity
        - ham_block[1]
        - sigma_pair[1]
        - product(coupling_block.T, inverse_coupled)
    )
    right_green = invert(right_matrix, energy, sweeps)
    left_green = left_inverse + product(product(inverse_coupled, right_green), coupled_inverse)
    return jnp.stack([left_green, right_green])


def lorentz(offset):
    scaled = offset / BROADENING
    return 1.0 / (1.0 + scaled * scaled)


def build_kernel(row_energy, column_energy):
    spacing = row_energy[:, None] - column_energy[None, :]
    kernel = lorentz(spacing - PHONON) + lorentz(spacing + PHONON)
    return kernel / jnp.sum(kernel, axis=1, keepdims=True)


def plain_body(sigma_in, hamiltonian, coupling, energies, counts, strengths, offsets):
    points = sigma_in.shape[0]
    order = sigma_in.shape[3]
    ranks = lax.axis_size("energy")
    moments = lax.axis_size("mom")
    my_rank = lax.axis_index("energy")
    own_energy = lax.dynamic_slice_in_dim(energies, my_rank * points, points)
    own_count = lax.dynamic_slice_in_dim(counts, my_rank * points, points)
    blocks = sigma_in[:, 0]

    def solve_held(held_point):
        return solve_point(hamiltonian[0], coupling[0], held_point[0], held_point[1], held_point[2])

    green_blocks = lax.map(solve_held, (blocks, own_energy, own_count))
    shift_index = jnp.arange(moments, dtype=jnp.int32)
    weights = jnp.sum(
        strengths[:, None] * (offsets[:, None] == shift_index[None, :]).astype(jnp.float32), axis=0
    )
    kernel = build_kernel(energies, energies)
    piece_width = 2 * order * order // ranks
    spread = green_blocks.reshape(points, ranks, moments, piece_width // moments)
    column = lax.all_to_all(spread, "energy", split_axis=1, concat_axis=0, tiled=True)[:, 0]
    rows_all = column.shape[0]
    flat_column = column.reshape(rows_all, -1)
    mixed_sum = weights[0] * flat_column
    for offset_step in range(1, moments):
        mixed_sum = mixed_sum + weights[offset_step] * shifted(flat_column, "mom", offset_step)
    sigma_part = product(kernel, mixed_sum).reshape(column.shape)
    result = lax.all_to_all(sigma_part[:, None], "energy", split_axis=0, concat_axis=1, tiled=True)
    sigma_new = result.reshape(sigma_in.shape)
    return (1.0 - MIX_RATE) * sigma_in + MIX_RATE * sigma_new


SUBLANES = 8
TOGETHER = 1
MESH_ID = pl.DeviceIdType.MESH


def split(value):
    high = value.astype(jnp.bfloat16)
    return high, (value - high.astype(jnp.float32)).astype(jnp.bfloat16)


def left_parts(value):
    high, low = split(value)
    return jnp.concatenate([high, low, high], axis=1)


def right_parts(value):
    high, low = split(value)
    return jnp.concatenate([high, high, low], axis=0)


def multiply(left_side, right_side):
    return jnp.dot(left_side, right_side, preferred_element_type=jnp.float32)


def series(ratios, energies, counts, identity):
    order = identity.shape[0]
    squares = [multiply(left_parts(r), right_parts(r)) for r in ratios]
    totals = [identity + r for r in ratios]
    for sweep in (1, 2, 3):
        rights = [right_parts(s) for s in squares]
        if sweep < 3:
            both = [
                multiply(jnp.concatenate([left_parts(t), left_parts(s)], axis=0), q)
                for t, s, q in zip(totals, squares, rights)
            ]
            added = [b[:order] for b in both]
            squares = [b[order:] for b in both]
        else:
            added = [multiply(left_parts(t), q) for t, q in zip(totals, rights)]
        totals = [jnp.where(sweep < c, t + a, t) for t, a, c in zip(totals, added, counts)]
    return [t * (1.0 / e) for t, e in zip(totals, energies)]


def kernel(
    ranks, moments, points, order, held,
    energy_ref, count_ref, strength_ref, offset_ref, sigma_hbm, ham_ref, coupling_ref,
    out_ref,
    green, gathered, mixed_out, wide, across, across_t,
    sigma_ref, read_sem, send_first, recv_first, send_second, recv_second,
):
    devices = ranks * moments
    total = ranks * points
    my_rank = lax.axis_index("energy")
    my_moment = lax.axis_index("mom")
    me = my_rank * moments + my_moment
    reads = [
        pltpu.make_async_copy(sigma_hbm.at[point], sigma_ref.at[point], read_sem.at[point])
        for point in range(points)
    ]
    for read in reads:
        read.start()
    barrier = pltpu.get_barrier_semaphore()

    def greet(index, carried):
        other = lax.rem(me + index, devices)
        pl.semaphore_signal(
            barrier, inc=1,
            device_id={"energy": other // moments, "mom": lax.rem(other, moments)},
            device_id_type=MESH_ID,
        )
        return carried

    lax.fori_loop(1, devices, greet, 0)

    across[...] = right_parts(coupling_ref[...])
    across_t[...] = left_parts(coupling_ref[...].T)
    row_index = lax.broadcasted_iota(jnp.int32, (order, order), 0)
    identity = (row_index == lax.broadcasted_iota(jnp.int32, (order, order), 1)).astype(jnp.float32)

    def place_of(other):
        return {"energy": other // moments, "mom": lax.rem(other, moments)}

    def give_first(source, landing, piece):
        pltpu.make_async_copy(source(me), landing, recv_first.at[piece]).start()

        def give(index, carried):
            other = lax.rem(me + index, devices)
            pltpu.make_async_remote_copy(
                src_ref=source(other),
                dst_ref=landing,
                send_sem=send_first,
                recv_sem=recv_first.at[piece],
                device_id=place_of(other),
                device_id_type=MESH_ID,
            ).start()
            return carried

        lax.fori_loop(1, devices, give, 0)

    def solve(group, carried):
        chosen = [group * TOGETHER + index for index in range(TOGETHER)]
        for point in chosen:
            pltpu.make_async_copy(sigma_hbm.at[point], sigma_ref.at[point], read_sem.at[point]).wait()
        energies = [energy_ref[my_rank * points + point] for point in chosen]
        counts = [count_ref[my_rank * points + point] for point in chosen]
        ratios = [(ham_ref[0] + sigma_ref[point, 0]) * (1.0 / e) for point, e in zip(chosen, energies)]
        left_inverses = series(ratios, energies, counts, identity)
        coupled = [multiply(left_parts(x), across[...]) for x in left_inverses]
        backs = [multiply(across_t[...], right_parts(x)) for x in left_inverses]
        folds = [multiply(across_t[...], right_parts(x)) for x in coupled]
        ratios = [
            (ham_ref[1] + sigma_ref[point, 1] + fold) * (1.0 / e)
            for point, e, fold in zip(chosen, energies, folds)
        ]
        right_greens = series(ratios, energies, counts, identity)
        inner = [multiply(left_parts(c), right_parts(x)) for c, x in zip(coupled, right_greens)]
        left_greens = [
            x + multiply(left_parts(i), right_parts(b)) for x, i, b in zip(left_inverses, inner, backs)
        ]
        tiles = order // SUBLANES
        for point, left_green, right_green in zip(chosen, left_greens, right_greens):
            green[point, :tiles] = left_green.reshape(tiles, SUBLANES, order)
            green[point, tiles:] = right_green.reshape(tiles, SUBLANES, order)

        @pl.when(group == 0)
        def _():
            pl.semaphore_wait(barrier, devices - 1)

        for point in chosen:
            landing = gathered.at[my_moment, 0, my_rank * points + point]
            give_first(lambda other: green.at[point, other * held], landing, 0)
        return carried

    lax.fori_loop(0, points // TOGETHER, solve, 0)

    for piece in range(1, held):
        landing = gathered.at[my_moment, piece, pl.ds(my_rank * points, points)]
        give_first(lambda other: green.at[:, other * held + piece], landing, piece)

    span = total * SUBLANES
    column = lax.broadcasted_iota(jnp.int32, (SUBLANES, span), 1)
    lane_slot = lax.rem(column, SUBLANES)
    lane_point = lax.div(column, SUBLANES)
    same = lane_slot == lax.broadcasted_iota(jnp.int32, (SUBLANES, span), 0)

    def place(index, carried):
        return jnp.where(lane_point == index, energy_ref[index], carried)

    column_energy = lax.fori_loop(0, total, place, jnp.zeros((SUBLANES, span), jnp.float32))

    def build(index, carried):
        spacing = energy_ref[index] - column_energy
        row = lorentz(spacing - PHONON) + lorentz(spacing + PHONON)
        row = jnp.where(same, row, 0.0)
        row = row * (MIX_RATE / jnp.sum(row, axis=1, keepdims=True))
        wide[pl.ds(pl.multiple_of(index * SUBLANES, SUBLANES), SUBLANES), :] = row
        return carried

    lax.fori_loop(0, total, build, 0)
    weights = []
    for step in range(moments):
        weight = jnp.float32(0.0)
        for transfer in range(strength_ref.shape[0]):
            weight = weight + jnp.where(offset_ref[transfer] == step, strength_ref[transfer], 0.0)
        weights.append(weight)

    wide_parts = left_parts(wide[...])
    for piece in range(held):
        arrived = gathered.at[:, piece]
        pltpu.make_async_copy(arrived, arrived, recv_first.at[piece]).wait()
        for turn in range(moments):
            moment = lax.rem(my_moment + 1 + turn, moments)
            scattered = weights[0] * gathered[moment, piece]
            for step in range(1, moments):
                source = lax.rem(moment - step + moments, moments)
                scattered = scattered + weights[step] * gathered[source, piece]
            result = multiply(wide_parts, right_parts(scattered.reshape(span, order)))
            mixed_out[moment, piece] = result.reshape(total, SUBLANES, order)

            def give_back(index, carried, moment=moment, piece=piece):
                rank = lax.rem(my_rank + index, ranks)
                pltpu.make_async_remote_copy(
                    src_ref=mixed_out.at[moment, piece, pl.ds(rank * points, points)],
                    dst_ref=out_ref.at[:, me * held + piece],
                    send_sem=send_second,
                    recv_sem=recv_second,
                    device_id={"energy": rank, "mom": moment},
                    device_id_type=MESH_ID,
                ).start()
                return carried

            if turn < moments - 1:
                lax.fori_loop(0, ranks, give_back, 0)
            else:
                lax.fori_loop(1, ranks, give_back, 0)
                pltpu.make_async_copy(
                    mixed_out.at[my_moment, piece, pl.ds(my_rank * points, points)],
                    out_ref.at[:, me * held + piece],
                    recv_second,
                ).start()

    pltpu.make_async_copy(out_ref, out_ref, recv_second).wait()
    sent = green.at[:, pl.ds(0, (devices - 1) * held)]
    pltpu.make_async_copy(sent, sent, send_first).wait()
    pltpu.make_async_copy(sent, sent, send_second).wait()


def fused_body(sigma_in, hamiltonian, coupling, energies, counts, strengths, offsets):
    points, order = sigma_in.shape[0], sigma_in.shape[3]
    ranks = lax.axis_size("energy")
    moments = lax.axis_size("mom")
    tiles = 2 * order // SUBLANES
    held = tiles // (ranks * moments)
    span = ranks * points * SUBLANES
    smem = pl.BlockSpec(memory_space=pltpu.SMEM)
    vmem = pl.BlockSpec(memory_space=pltpu.VMEM)
    sigma_new = pl.pallas_call(
        functools.partial(kernel, ranks, moments, points, order, held),
        out_shape=jax.ShapeDtypeStruct((points, tiles, SUBLANES, order), jnp.float32),
        in_specs=[smem] * 4 + [pl.BlockSpec(memory_space=pl.ANY)] + [vmem] * 2,
        out_specs=pl.BlockSpec(memory_space=pl.ANY),
        scratch_shapes=[
            pltpu.VMEM((points, tiles, SUBLANES, order), jnp.float32),
            pltpu.VMEM((moments, held, ranks * points, SUBLANES, order), jnp.float32),
            pltpu.VMEM((moments, held, ranks * points, SUBLANES, order), jnp.float32),
            pltpu.VMEM((span, span), jnp.float32),
            pltpu.VMEM((3 * order, order), jnp.bfloat16),
            pltpu.VMEM((order, 3 * order), jnp.bfloat16),
            pltpu.VMEM((points, 2, order, order), jnp.float32),
            pltpu.SemaphoreType.DMA((points,)),
            pltpu.SemaphoreType.DMA,
            pltpu.SemaphoreType.DMA((held,)),
            pltpu.SemaphoreType.DMA,
            pltpu.SemaphoreType.DMA,
        ],
        compiler_params=pltpu.CompilerParams(
            collective_id=0, has_side_effects=True, vmem_limit_bytes=60 * 1024 * 1024
        ),
        name="green_and_scatter",
    )(energies, counts, strengths, offsets, sigma_in[:, 0], hamiltonian[0], coupling[0])
    return (1.0 - MIX_RATE) * sigma_in + sigma_new.reshape(sigma_in.shape)


def body(sigma_in, hamiltonian, coupling, energies, counts, strengths, offsets):
    devices = lax.axis_size("energy") * lax.axis_size("mom")
    tiles = 2 * sigma_in.shape[3] // SUBLANES
    fits = tiles % devices == 0 and devices % 2 == 0 and sigma_in.shape[0] % TOGETHER == 0
    chosen = fused_body if fits else plain_body
    return chosen(sigma_in, hamiltonian, coupling, energies, counts, strengths, offsets)


def solution(mesh):
    placed = (
        P("energy", "mom", None, None, None),
        P("mom", None, None, None),
        P("mom", None, None),
        P(),
        P(),
        P(),
        P(),
    )
    return jax.shard_map(
        body,
        mesh=mesh,
        in_specs=placed,
        out_specs=P("energy", "mom", None, None, None),
        check_vma=False,
    )
```
